32 devices in a mesh: dp: 8 (over z, x), rep: 4 (over y, core).
Axes of the slice: x: 2, y: 2, z: 4, core: 2. Of those that a mesh axis runs over, the one named last changes fastest.
Arguments:
- hot_ids: int32 [8192, 2], P(('dp', 'rep')), may hold values from 0 to 1023
- cold_owner: int32 [16384, 1], P(('dp', 'rep')), may hold values from 0 to 7; in each aligned block of 512 rows (0 to 511, 512 to 1023, ...) at most 128 rows name the same one
- cold_offset: int32 [16384], P(('dp', 'rep')), may hold values from 0 to 511
- labels: int32 [8192], P(('dp', 'rep')), may hold values 0 or 1
- top_weight: bfloat16 [512, 1024], replicated, may hold values from -0.25 to 0.25
- out_weight: float32 [1024], replicated, may hold values from -0.5 to 0.5
- cold_table: float32 [4096, 128], P('dp'), may hold values from -6 to 6
- cold_accum: float32 [4096, 128], P('dp'), may hold values from 0.0001 to 0.01
- hot_cache: float32 [1024, 128], replicated, may hold values from -6 to 6
- hot_accum: float32 [1024, 128], replicated, may hold values from 0.01 to 1
- pending: float32 [32768, 128], P(('dp', 'rep')), may hold values from -0.3 to 0.3
- refresh_blocks: int32 [3], replicated, may hold values from 0 to 7, as said below
- block_clock: int32 [8], replicated, may hold values from 0 to 8
Outputs:
- cold_table_new: float32 [4096, 128], P('dp')
- cold_accum_new: float32 [4096, 128], P('dp')
- hot_cache_new: float32 [1024, 128], replicated
- hot_accum_new: float32 [1024, 128], replicated
- pending_new: float32 [32768, 128], P(('dp', 'rep'))
- top_grad: float32 [512, 1024], P(('dp', 'rep'))
- out_grad: float32 [1024], replicated
The draws below stay inside these ranges and needn't reach their ends.
Inputs may be any that keep to these rules, and one draw needn't show every extreme that they name: `cold_owner`: within the lookups of one device (512 rows), no owner is named more than 128 times. `refresh_blocks`: the block numbers are distinct.
All inputs are finite; a program needn't handle non-finite values. No bound on the sum of `labels` on one device may be relied on, other than what follows from the above.
Results may differ from the reference program's by a relative error of at most 0.00165.
The reference program's roundings to bfloat16 on the way (of `hot_rows`, `cold_rows`, `inputs`, `hidden`, `dhidden` and `dinputs`) count: a program that leaves them out, or rounds other values in their place, can miss the bound.
Values may be sent and summed in bfloat16 or wider, within the bound.
A program may use at most 64 MiB of HBM per device.

```python
import math
import jax
import jax.numpy as jnp
import numpy as np
from jax import lax

E = 128
H = 1024
FH = 2
FC = 2
B_DEV = 256
OWN_ROWS = 512
BLOCK = 128
HBLK = 8
NREF = 3
HOT = 1024
CAP = 128
SAMPLES = 8192
N_DP = 8
N_REP = 4


def draw_refresh_blocks(key, part):
    shuffled = jax.random.permutation(jax.random.fold_in(key, 41), HBLK)
    return shuffled[:NREF].astype(jnp.int32)


def place_ends(drawn, own_key, smallest, high):
    dims = drawn.shape
    spot = [jax.random.randint(jax.random.fold_in(own_key, axis), (), 0, dims[axis]) for axis in range(len(dims))]
    drawn = drawn.at[tuple(spot)].set(smallest)
    longest = dims.index(max(dims))
    spot[longest] = (spot[longest] + 1) % dims[longest]
    return drawn.at[tuple(spot)].set(high)


def level_of(rng, shape, cuts, low, high):
    factor_of = 1.0
    for dim, parts in cuts:
        heights = jax.random.uniform(jax.random.fold_in(jax.random.fold_in(rng, 6), dim), (parts,), jnp.float32, low / len(cuts), high / len(cuts))
        factor_of = factor_of * jnp.repeat(jnp.exp(heights), shape[dim] // parts).reshape((-1,) + (1,) * (len(shape) - 1 - dim))
    return factor_of


def rank_bounds(number_of, skew):
    weights = [(1 << 20) // math.isqrt(standing ** skew) + 1 for standing in range(1, number_of + 1)]
    spread = 1 + sum(weights) // (1 << 30)
    return np.cumsum(np.array([max(1, weight // spread) for weight in weights]))


def ranked_ids(rng, shape, count, skew):
    table = rank_bounds(count, skew)
    pick = jax.random.randint(jax.random.fold_in(rng, 1), shape, 0, int(table[count - 1]))
    grade = jnp.searchsorted(jnp.asarray(table, jnp.int32), pick, side="right")
    return jax.random.permutation(jax.random.fold_in(rng, 2), count)[grade].astype(jnp.int32)


def shared_out(rng, own, number, rows, count, top, most, skew):
    ranking = jax.random.permutation(rng, count)
    crowded, usual = shares(count, rows * top, most, skew, True), shares(count, rows * top, most, skew, False)
    places = jnp.arange(count)

    def named(tallies, offset_by):
        used = int((tallies > 0).sum())
        fixed = max(1, used // 4)
        passed = fixed + (places - fixed + offset_by * (used - fixed)) % max(1, count - fixed)
        return jnp.zeros((count,), jnp.int32).at[ranking[jnp.where(places < fixed, places, passed)]].set(jnp.asarray(tallies, jnp.int32))

    tallies = jnp.where(number % 4 == 0, named(crowded, number // 4), named(usual, number - number // 4 - 1))
    mixed = jax.random.permutation(jax.random.fold_in(own, 3), count)
    giver, receiver = mixed[0:count // 2 * 2:2], mixed[1:count // 2 * 2:2]
    margin = jnp.minimum(tallies[giver] - 1, most - tallies[receiver]) // 2
    margin = jnp.where((giver == ranking[0]) | (receiver == ranking[0]) | (tallies[receiver] == 0), 0, jnp.maximum(margin, 0))
    passed = jax.random.randint(jax.random.fold_in(own, 4), (count // 2,), 0, 1 << 20) % (margin + 1)
    tallies = tallies.at[giver].add(-passed).at[receiver].add(passed)
    items = jnp.searchsorted(jnp.cumsum(tallies), jnp.arange(rows * top), side="right").astype(jnp.int32)
    listing = items.reshape(top, rows).T
    listing = listing[jax.random.permutation(jax.random.fold_in(own, 1), rows)]
    offset_by = jax.random.randint(jax.random.fold_in(own, 2), (rows, 1), 0, top)
    return jnp.take_along_axis(listing, (jnp.arange(top)[None, :] + offset_by) % top, axis=1)


def shares(count, total, reach, skew, full):
    loads = [(1 << 20) // math.isqrt(rank ** skew) + 1 for rank in range(1, count + 1)]
    largest = reach if full else min(reach, max(-(-total // count), total * loads[0] // sum(loads)))
    least = 1 if total - largest >= count - 1 else 0
    holding, surplus = [largest] + [least] * (count - 1), total - largest - least * (count - 1)
    while surplus > 0:
        free = [i for i in range(1, count) if holding[i] < largest] or [i for i in range(1, count) if holding[i] < reach]
        pool, remaining = sum([loads[i] for i in free]), surplus
        for i in free:
            extra = min(reach - holding[i], max(1, remaining * loads[i] // pool), surplus)
            holding[i] = holding[i] + extra
            surplus = surplus - extra
    return np.array(holding)


def normal_values(own_key, dims, scale, limit, cuts=(), kind=jnp.bfloat16):
    factor_of = level_of(own_key, dims, cuts, -0.22, 0.18) if cuts else 1.0
    array = jax.random.normal(own_key, dims, jnp.float32) * scale * factor_of
    return jnp.minimum(jnp.maximum(array, -limit), limit).astype(kind)


def setup_inputs(seed: int = 0) -> dict:
    key_of = jax.random.split(jax.random.key(seed), 14)
    hot_ids = place_ends(ranked_ids(key_of[0], (SAMPLES, FH), HOT, 2), jax.random.fold_in(key_of[0], 3), 0, HOT - 1).astype(jnp.int32)
    cold_owner_keys = jax.random.split(jax.random.fold_in(key_of[1], 1), (SAMPLES * FC) // (B_DEV * FC))
    cold_owner_turns = jax.random.permutation(jax.random.fold_in(key_of[1], 3), (SAMPLES * FC) // (B_DEV * FC))
    cold_owner = jax.vmap(lambda own, number: shared_out(jax.random.fold_in(key_of[1], 2), own, number, B_DEV * FC, N_DP, 1, CAP, 2))(cold_owner_keys, cold_owner_turns).reshape((SAMPLES * FC, 1))
    cold_offset = place_ends(jax.random.randint(key_of[2], (SAMPLES * FC,), 0, OWN_ROWS), jax.random.fold_in(key_of[2], 1), 0, OWN_ROWS - 1).astype(jnp.int32)
    labels = place_ends((jax.random.randint(key_of[3], (SAMPLES,), 0, 2) < 1).astype(jnp.int32), jax.random.fold_in(key_of[3], 1), 0, 1)
    top_weight = normal_values(key_of[4], ((FH + FC) * E, H), ((FH + FC) * E) ** -0.5, 0.25)
    out_weight = normal_values(key_of[5], (H,), (H // 8) ** -0.5, 0.5, (), jnp.float32)
    cold_table = normal_values(key_of[6], (N_DP * OWN_ROWS, E), 1.0, 6.0, ((0, 8),), jnp.float32)
    cold_accum = jnp.clip(jnp.exp(math.log(0.01) - 4.6051702 * jax.random.uniform(key_of[7], (N_DP * OWN_ROWS, E), jnp.float32) ** level_of(key_of[7], (N_DP * OWN_ROWS, E), ((0, 8),), -0.2, 0.2)), 0.0001, 0.01)
    hot_cache = normal_values(key_of[8], (HOT, E), 1.0, 6.0, (), jnp.float32)
    hot_accum = jnp.clip(jnp.exp(jax.random.uniform(key_of[9], (HOT, E), jnp.float32, math.log(0.01), math.log(1.0))), 0.01, 1.0)
    pending = normal_values(key_of[10], (N_DP * N_REP * HOT, E), 0.05, 0.3, ((0, 32),), jnp.float32)
    refresh_blocks = draw_refresh_blocks(jax.random.fold_in(key_of[13], 71), 0)
    block_clock = place_ends(jax.random.randint(key_of[12], (HBLK,), 0, 9), jax.random.fold_in(key_of[12], 1), 0, 8).astype(jnp.int32)
    return dict(hot_ids=hot_ids, cold_owner=cold_owner, cold_offset=cold_offset, labels=labels, top_weight=top_weight, out_weight=out_weight, cold_table=cold_table, cold_accum=cold_accum, hot_cache=hot_cache, hot_accum=hot_accum, pending=pending, refresh_blocks=refresh_blocks, block_clock=block_clock)


step_size = 0.5
epsilon = 1e-08

def adagrad(table_rows, accum_rows, gradient):
    accum_next = accum_rows + gradient * gradient
    return (table_rows - step_size * gradient / (jnp.sqrt(accum_next) + epsilon), accum_next)

def reference(hot_ids, cold_owner, cold_offset, labels, top_weight, out_weight, cold_table, cold_accum, hot_cache, hot_accum, pending, refresh_blocks, block_clock):
    devices = N_DP * N_REP
    samples = hot_ids.shape[0]
    width = hot_cache.shape[1]
    hot_rows = hot_cache[hot_ids].astype(jnp.bfloat16)
    global_rows = (cold_owner[:, 0] * OWN_ROWS + cold_offset).astype(jnp.int32)
    cold_rows = cold_table[global_rows].astype(jnp.bfloat16).reshape(samples, FC, width)
    inputs = jnp.concatenate([hot_rows, cold_rows], axis=1).reshape(samples, (FH + FC) * width)
    groups = N_DP
    inputs_grouped = inputs.reshape(groups, samples // groups, (FH + FC) * width)
    labels_grouped = labels.reshape(groups, samples // groups).astype(jnp.float32)

    def per_group(carry, pieces):
        block_inputs, block_labels = pieces
        preact = jnp.dot(block_inputs, top_weight, preferred_element_type=jnp.float32)
        hidden = jax.nn.silu(preact).astype(jnp.bfloat16)
        hidden_wide = hidden.astype(jnp.float32)
        logits = jnp.dot(hidden_wide, out_weight, precision=lax.Precision.HIGHEST)
        errors = jax.nn.sigmoid(logits) - block_labels
        gates = jax.nn.sigmoid(preact)
        slope = gates * (1.0 + preact * (1.0 - gates))
        dhidden = (errors[:, None] * out_weight[None, :] * slope).astype(jnp.bfloat16)
        weight_term = lax.dot_general(block_inputs, dhidden, (((0,), (0,)), ((), ())), preferred_element_type=jnp.float32)
        head_term = jnp.dot(errors, hidden_wide, precision=lax.Precision.HIGHEST)
        dinputs = lax.dot_general(dhidden, top_weight, (((1,), (1,)), ((), ())), preferred_element_type=jnp.float32).astype(jnp.bfloat16)
        return ((carry[0] + weight_term, carry[1] + head_term), dinputs)
    start = (jnp.zeros(top_weight.shape, jnp.float32), jnp.zeros(out_weight.shape, jnp.float32))
    totals, dinputs = lax.scan(per_group, start, (inputs_grouped, labels_grouped))
    top_grad, out_grad = totals
    dinputs = dinputs.reshape(samples, FH + FC, width)
    hot_dx = dinputs[:, :FH].reshape(samples * FH, width).astype(jnp.float32)
    cold_dx = dinputs[:, FH:].reshape(samples * FC, width).astype(jnp.float32)
    cold_grad = jnp.zeros(cold_table.shape, jnp.float32).at[global_rows].add(cold_dx)
    cold_table_new, cold_accum_new = adagrad(cold_table, cold_accum, cold_grad)
    device_of = (jnp.arange(samples) // (samples // devices)).astype(jnp.int32)
    hot_index = (device_of[:, None] * HOT + hot_ids).astype(jnp.int32).reshape(-1)
    hot_grad = jnp.zeros(pending.shape, jnp.float32).at[hot_index].add(hot_dx)
    carried = (pending + hot_grad).reshape(devices, HBLK, BLOCK, width)
    picked = lax.optimization_barrier(jnp.sum(carried[:, refresh_blocks], axis=0))
    divisors = 1.0 + block_clock[refresh_blocks].astype(jnp.float32)
    flush = picked / divisors[:, None, None]
    cache_blocks = hot_cache.reshape(HBLK, BLOCK, width)
    accum_blocks = hot_accum.reshape(HBLK, BLOCK, width)
    cache_part, accum_part = adagrad(cache_blocks[refresh_blocks], accum_blocks[refresh_blocks], flush)
    hot_cache_new = cache_blocks.at[refresh_blocks].set(cache_part).reshape(HOT, width)
    hot_accum_new = accum_blocks.at[refresh_blocks].set(accum_part).reshape(HOT, width)
    pending_new = carried.at[:, refresh_blocks].set(0.0).reshape(devices * HOT, width)
    return (cold_table_new, cold_accum_new, hot_cache_new, hot_accum_new, pending_new, top_grad, out_grad)
```

```python
import functools

import jax
import jax.numpy as jnp
from jax import lax
from jax.experimental import pallas as pl
from jax.experimental.pallas import tpu as pltpu
from jax.sharding import PartitionSpec as P

BLOCK = 128
MESH = pl.DeviceIdType.MESH


step_size = 0.5
epsilon = 1e-08


def adagrad(table_rows, accum_rows, gradient):
    accum_next = accum_rows + gradient * gradient
    return (table_rows - step_size * gradient / (jnp.sqrt(accum_next) + epsilon), accum_next)


def bit_of(index, weight):
    return lax.rem(lax.div(index, weight), 2)


def flipped(index, weight):
    return index + weight * (1 - 2 * bit_of(index, weight))


def greet(devices):
    barrier = pltpu.get_barrier_semaphore()
    for device in devices:
        pl.semaphore_signal(barrier, inc=1, device_id=device, device_id_type=MESH)
    pl.semaphore_wait(barrier, len(devices))


def chosen(offsets, rows):
    shape = (rows, offsets.shape[1])
    asks = lax.broadcasted_iota(jnp.int32, shape, 0) == jnp.broadcast_to(offsets, shape)
    return jnp.where(asks, 1.0, 0.0).astype(jnp.bfloat16)


def fetch_kernel(n, requests, table, asked_out, returned_out, asked, found, returned, sems):
    me, rep = lax.axis_index("dp"), lax.axis_index("rep")
    peers = [lax.rem(me + j, n) for j in range(1, n)]
    sources = [lax.rem(me + n - j, n) for j in range(1, n)]
    greet([(peer, rep) for peer in peers])
    asking = []
    for j, peer in enumerate(peers):
        copy = pltpu.make_async_remote_copy(
            requests.at[peer], asked.at[me], sems.at[0, j], sems.at[1, j], (peer, rep), MESH
        )
        copy.start()
        asking.append(copy)
    rows = table[...].astype(jnp.bfloat16)

    def rows_of(offsets):
        return lax.dot_general(
            chosen(offsets, rows.shape[0]),
            rows,
            (((0,), (0,)), ((), ())),
            preferred_element_type=jnp.float32,
        ).astype(jnp.bfloat16)

    asked[me] = requests[me]
    returned[me] = rows_of(requests[me])
    answers = []
    for j, source in enumerate(sources):
        asking[j].wait_recv()
        found[j] = rows_of(asked[source])
        copy = pltpu.make_async_remote_copy(
            found.at[j], returned.at[me], sems.at[2, j], sems.at[3, j], (source, rep), MESH
        )
        copy.start()
        answers.append(copy)
    asked_out[...] = asked[...]
    for j in range(n - 1):
        asking[j].wait_send()
        answers[j].wait()
    returned_out[...] = returned[...]


def fetch(requests, table):
    n, cap = requests.shape
    width = table.shape[1]
    vmem = pl.BlockSpec(memory_space=pltpu.VMEM)
    asked, returned = pl.pallas_call(
        functools.partial(fetch_kernel, n),
        out_shape=(
            jax.ShapeDtypeStruct((n, 1, cap), jnp.int32),
            jax.ShapeDtypeStruct((n, cap, width), jnp.bfloat16),
        ),
        in_specs=[vmem] * 2,
        out_specs=(vmem, vmem),
        scratch_shapes=[
            pltpu.VMEM((n, 1, cap), jnp.int32),
            pltpu.VMEM((n - 1, cap, width), jnp.bfloat16),
            pltpu.VMEM((n, cap, width), jnp.bfloat16),
            pltpu.SemaphoreType.DMA((4, n - 1)),
        ],
        compiler_params=pltpu.CompilerParams(collective_id=0, has_side_effects=True),
    )(requests.reshape(n, 1, cap), table)
    return asked, returned


def combine_kernel(
    n, links, top, hot, outgoing, asked, table, accum,
    top_out, hot_out, table_out, accum_out,
    incoming, cold, cold_half, cold_got, cold_last, table_all, accum_all,
    top_got, a_parts, a_gots, b_parts, b_gots, h_parts, h_gots, h_news, sends, recvs,
):
    me, rep = lax.axis_index("dp"), lax.axis_index("rep")
    core, side = bit_of(rep, 1), bit_of(rep, 2)
    over_core, over_side = (me, flipped(rep, 1)), (me, flipped(rep, 2))
    weights = [1 << k for k in range(links)]
    dp_bits = [bit_of(me, weight) for weight in weights]
    over_dp = [(flipped(me, weight), rep) for weight in weights]
    peers = [lax.rem(me + j, n) for j in range(1, n)]
    sources = [lax.rem(me + n - j, n) for j in range(1, n)]
    greet([(peer, rep) for peer in peers] + [over_core, over_side])
    count = [0]

    def send(src, dst, device):
        k = count[0]
        count[0] += 1
        copy = pltpu.make_async_remote_copy(src, dst, sends.at[k], recvs.at[k], device, MESH)
        copy.start()
        return copy

    top_copy = send(top.at[:, 1 - core], top_got, over_core)
    cold_copies = [
        send(outgoing.at[peer], incoming.at[me], (peer, rep)) for peer in peers
    ]
    hot_copy = send(hot.at[:, 1 - core], h_gots[0], over_core)

    a_route = [(side, over_side)] + list(zip(dp_bits, over_dp))
    b_route = [(dp_bits[0], over_dp[0]), (side, over_side)] + list(zip(dp_bits, over_dp))[1:]
    h_route = [(core, over_core)] + a_route

    def step_on(parts, gots, route, k, copy):
        bit = route[k][0]
        copy.wait()
        kept = parts[k][:, bit] + gots[k][...]
        if k + 1 == len(route):
            return kept
        parts[k + 1][...] = kept.reshape(parts[k + 1].shape)
        next_bit, device = route[k + 1]
        return send(parts[k + 1].at[:, 1 - next_bit], gots[k + 1], device)

    top_copy.wait()
    half = top.shape[3] // 2
    a_parts[0][...] = (top[:, core, :, :half] + top_got[:, :, :half]).reshape(a_parts[0].shape)
    a_copy = send(a_parts[0].at[:, 1 - side], a_gots[0], over_side)
    b_parts[0][...] = (top[:, core, :, half:] + top_got[:, :, half:]).reshape(b_parts[0].shape)
    b_copy = send(b_parts[0].at[:, 1 - dp_bits[0]], b_gots[0], over_dp[0])
    all_h = [hot] + list(h_parts)
    hot_copy = step_on(all_h, h_gots, h_route, 0, hot_copy)

    own_rows = 4 * table.shape[0]
    total = jnp.dot(
        chosen(asked[me], own_rows), outgoing[me], preferred_element_type=jnp.float32
    )
    for j, source in enumerate(sources):
        cold_copies[j].wait_recv()
        total += jnp.dot(
            chosen(asked[source], own_rows), incoming[source], preferred_element_type=jnp.float32
        )
    cold[...] = total.reshape(cold.shape)
    cold_copy = send(cold.at[:, 1 - core], cold_got, over_core)
    hot_copy = step_on(all_h, h_gots, h_route, 1, hot_copy)
    cold_copy.wait()
    cold_half[...] = cold[:, core] + cold_got[...]
    cold_copy = send(cold_half.at[1 - side], cold_last, over_side)
    a_copy = step_on(a_parts, a_gots, a_route, 0, a_copy)
    b_copy = step_on(b_parts, b_gots, b_route, 0, b_copy)
    hot_copy = step_on(all_h, h_gots, h_route, 2, hot_copy)
    cold_copy.wait()
    table_next, accum_next = adagrad(table[...], accum[...], cold_half[side] + cold_last[...])
    table_all[side, core] = table_next
    accum_all[side, core] = accum_next
    pair = [send(ref.at[side, core], ref.at[side, core], over_side) for ref in (table_all, accum_all)]
    last = len(a_route)
    for k in range(1, last):
        if k + 2 <= last:
            hot_copy = step_on(all_h, h_gots, h_route, k + 2, hot_copy)
        if k + 2 == last:
            cur = h_news[0]
            cur[...] = hot_copy
            bit, device = h_route[-1]
            hot_step = send(cur, h_news[1].at[:, bit], device)
            h_news[1][:, bit] = cur[...]
        a_copy = step_on(a_parts, a_gots, a_route, k, a_copy)
        b_copy = step_on(b_parts, b_gots, b_route, k, b_copy)
        if k == 1:
            for copy in pair:
                copy.wait()
            pair = [send(ref.at[:, core], ref.at[:, core], over_core) for ref in (table_all, accum_all)]
    top_out[:, :half] = a_copy.reshape(top_out.shape[0], half)
    top_out[:, half:] = b_copy.reshape(top_out.shape[0], half)
    for copy in pair:
        copy.wait()
    table_out[...] = table_all[...]
    accum_out[...] = accum_all[...]
    for k in range(len(h_route) - 2, -1, -1):
        hot_step.wait()
        stage = 2 * (len(h_route) - 2 - k)
        got, cur, new = h_news[stage + 1], h_news[stage + 2], h_news[stage + 3]
        cur[...] = got[...].reshape(cur.shape)
        bit, device = h_route[k]
        hot_step = send(cur, new.at[:, bit], device)
        new[:, bit] = cur[...]
    hot_step.wait()
    hot_out[...] = h_news[-1][...]
    for copy in cold_copies:
        copy.wait_send()


def combine(top, hot, outgoing, asked, table, accum):
    n, cap, width = outgoing.shape
    devices = 4 * n
    links = n.bit_length() - 1
    rows, columns = top.shape[0] // devices, top.shape[1]
    hot_rows = hot.shape[0] // devices
    quarter = table.shape[0]
    half = columns // 2
    f32 = lambda *shape: pltpu.VMEM(shape, jnp.float32)
    steps = [2**k for k in range(links, -1, -1)]
    a_parts = [f32(m, 2, rows, half) for m in steps]
    a_gots = [f32(m, rows, half) for m in steps]
    b_parts = [f32(n // 2, 2, 2, rows, half), f32(n // 2, 2, rows, half)] + a_parts[2:]
    b_gots = [f32(n // 2, 2, rows, half), f32(n // 2, rows, half)] + a_gots[2:]
    h_parts = [f32(m, 2, hot_rows, width) for m in steps]
    h_gots = [f32(m, hot_rows, width) for m in [2 * n] + steps]
    h_news = []
    for m in steps[::-1] + [2 * n]:
        h_news += [f32(m, hot_rows, width), f32(m, 2, hot_rows, width)]
    copies = 1 + (n - 1) + 2 * (links + 1) + 2 * (links + 2) + 2 + 4
    vmem = pl.BlockSpec(memory_space=pltpu.VMEM)
    out = lambda *shape: jax.ShapeDtypeStruct(shape, jnp.float32)
    square = (2, 2, quarter, width)
    return pl.pallas_call(
        functools.partial(combine_kernel, n, links),
        out_shape=(
            out(rows, columns), out(2 * n, 2, hot_rows, width), out(*square), out(*square)
        ),
        in_specs=[vmem] * 6,
        out_specs=(vmem,) * 4,
        scratch_shapes=[
            pltpu.VMEM((n, cap, width), jnp.bfloat16),
            f32(*square),
            f32(2, quarter, width),
            f32(2, quarter, width),
            f32(quarter, width),
            f32(*square),
            f32(*square),
            f32(2 * n, rows, columns),
            a_parts, a_gots, b_parts, b_gots, h_parts, h_gots, h_news,
            pltpu.SemaphoreType.DMA((copies,)),
            pltpu.SemaphoreType.DMA((copies,)),
        ],
        compiler_params=pltpu.CompilerParams(collective_id=1, has_side_effects=True),
    )(
        top.reshape(2 * n, 2, rows, columns),
        hot.reshape(2 * n, 2, hot_rows, width),
        outgoing, asked, table, accum,
    )


def suits(n, rep_n, top_rows):
    return rep_n == 4 and n >= 2 and n & (n - 1) == 0 and top_rows % (8 * n * rep_n) == 0


def local(
    hot_ids,
    cold_owner,
    cold_offset,
    labels,
    top_weight,
    out_weight,
    cold_table,
    cold_accum,
    hot_cache,
    hot_accum,
    pending,
    refresh_blocks,
    block_clock,
):
    width = hot_cache.shape[1]
    samples = hot_ids.shape[0]
    hot_feats = hot_ids.shape[1]
    lookups = cold_offset.shape[0]
    cold_feats = lookups // samples
    owners_count = lax.axis_size("dp")
    capacity = max(2, 2 * lookups // owners_count)
    owners = cold_owner[:, 0]
    matches = (owners[:, None] == jnp.arange(owners_count, dtype=jnp.int32)[None, :]).astype(
        jnp.int32
    )
    earlier = jnp.cumsum(matches, axis=0) - matches
    positions = jnp.sum(earlier * matches, axis=1)
    targets = owners * capacity + positions
    requests = jnp.zeros((owners_count * capacity,), jnp.int32).at[targets].set(cold_offset)
    requests = requests.reshape(owners_count, capacity)
    direct = suits(owners_count, lax.axis_size("rep"), top_weight.shape[0])
    if direct:
        asked, returned = fetch(requests, cold_table)
    else:
        asked = lax.all_to_all(requests, "dp", split_axis=0, concat_axis=0, tiled=True)
        found = cold_table[asked].astype(jnp.bfloat16)
        returned = lax.all_to_all(found, "dp", split_axis=0, concat_axis=0, tiled=True)
    cold_rows = returned.reshape(owners_count * capacity, width)[targets]
    cold_rows = cold_rows.reshape(samples, cold_feats, width)
    hot_rows = hot_cache[hot_ids].astype(jnp.bfloat16)
    inputs = jnp.concatenate([hot_rows, cold_rows], axis=1).reshape(
        samples, (hot_feats + cold_feats) * width
    )
    preact = jnp.dot(inputs, top_weight, preferred_element_type=jnp.float32)
    hidden = jax.nn.silu(preact).astype(jnp.bfloat16)
    hidden_wide = hidden.astype(jnp.float32)
    logits = jnp.dot(hidden_wide, out_weight, precision=lax.Precision.HIGHEST)
    errors = jax.nn.sigmoid(logits) - labels.astype(jnp.float32)
    gates = jax.nn.sigmoid(preact)
    slope = gates * (1.0 + preact * (1.0 - gates))
    dhidden = (errors[:, None] * out_weight[None, :] * slope).astype(jnp.bfloat16)
    head_term = jnp.dot(errors, hidden_wide, precision=lax.Precision.HIGHEST)
    top_part = lax.dot_general(
        inputs, dhidden, (((0,), (0,)), ((), ())), preferred_element_type=jnp.float32
    )
    dinputs = lax.dot_general(
        dhidden, top_weight, (((1,), (1,)), ((), ())), preferred_element_type=jnp.float32
    ).astype(jnp.bfloat16)
    dinputs = dinputs.reshape(samples, hot_feats + cold_feats, width)
    cold_dx = dinputs[:, hot_feats:].reshape(lookups, width)
    outgoing = jnp.zeros((owners_count * capacity, width), jnp.bfloat16).at[targets].set(cold_dx)
    outgoing = outgoing.reshape(owners_count, capacity, width)
    own_rows = cold_table.shape[0]
    quarter = own_rows // lax.axis_size("rep")
    offset_rows = lax.axis_index("rep") * quarter
    table_share = lax.dynamic_slice_in_dim(cold_table, offset_rows, quarter, 0)
    accum_share = lax.dynamic_slice_in_dim(cold_accum, offset_rows, quarter, 0)
    hot_count = hot_cache.shape[0]
    blocks_count = hot_count // BLOCK
    hot_dx = dinputs[:, :hot_feats].reshape(samples * hot_feats, width)
    hot_named = (
        jnp.arange(hot_count, dtype=jnp.int32)[:, None] == hot_ids.reshape(-1)[None, :]
    ).astype(jnp.bfloat16)
    hot_grad = jnp.dot(hot_named, hot_dx, preferred_element_type=jnp.float32)
    carried = (pending + hot_grad).reshape(blocks_count, BLOCK, width)
    picked = carried[refresh_blocks]
    divisors = 1.0 + block_clock[refresh_blocks].astype(jnp.float32)
    cache_blocks = hot_cache.reshape(blocks_count, BLOCK, width)
    accum_blocks = hot_accum.reshape(blocks_count, BLOCK, width)
    cache_chosen = cache_blocks[refresh_blocks]
    accum_chosen = accum_blocks[refresh_blocks]
    if direct:
        picked_rows = refresh_blocks.shape[0] * BLOCK
        head_rows = head_term.shape[0] // width
        even = 8 * owners_count * lax.axis_size("rep")
        spare = -(picked_rows + head_rows) % even
        summands = jnp.concatenate(
            [
                picked.reshape(picked_rows, width),
                head_term.reshape(head_rows, width),
                jnp.zeros((spare, width), jnp.float32),
            ]
        )
        top_grad, sums, cold_table_new, cold_accum_new = combine(
            top_part, summands, outgoing, asked, table_share, accum_share
        )
        cold_table_new = cold_table_new.reshape(own_rows, width)
        cold_accum_new = cold_accum_new.reshape(own_rows, width)
        sums = sums.reshape(-1, width)
        picked_sum = sums[:picked_rows].reshape(picked.shape)
        out_grad = sums[picked_rows : picked_rows + head_rows].reshape(-1)
    else:
        incoming = lax.all_to_all(outgoing, "dp", split_axis=0, concat_axis=0, tiled=True)
        cold_grad = (
            jnp.zeros((own_rows, width), jnp.float32)
            .at[asked.reshape(-1)]
            .add(incoming.reshape(-1, width).astype(jnp.float32))
        )
        cold_share = lax.psum_scatter(cold_grad, "rep", scatter_dimension=0, tiled=True)
        table_updated, accum_updated = adagrad(table_share, accum_share, cold_share)
        cold_table_new, cold_accum_new = (
            lax.all_gather(table_updated, "rep", axis=0, tiled=True),
            lax.all_gather(accum_updated, "rep", axis=0, tiled=True),
        )
        top_grad = lax.psum_scatter(top_part, ("dp", "rep"), scatter_dimension=0, tiled=True)
        picked_sum, out_grad = lax.psum((picked, head_term), ("dp", "rep"))
    flush = picked_sum / divisors[:, None, None]
    cache_part, accum_part = adagrad(cache_chosen, accum_chosen, flush)
    hot_cache_new = cache_blocks.at[refresh_blocks].set(cache_part).reshape(hot_count, width)
    hot_accum_new = accum_blocks.at[refresh_blocks].set(accum_part).reshape(hot_count, width)
    pending_new = carried.at[refresh_blocks].set(0.0).reshape(hot_count, width)
    return (
        cold_table_new,
        cold_accum_new,
        hot_cache_new,
        hot_accum_new,
        pending_new,
        top_grad,
        out_grad,
    )


def solution(mesh):
    in_specs = (
        P(("dp", "rep"), None),
        P(("dp", "rep"), None),
        P(("dp", "rep")),
        P(("dp", "rep")),
        P(),
        P(),
        P("dp", None),
        P("dp", None),
        P(),
        P(),
        P(("dp", "rep"), None),
        P(),
        P(),
    )
    out_specs = (
        P("dp", None),
        P("dp", None),
        P(),
        P(),
        P(("dp", "rep"), None),
        P(("dp", "rep"), None),
        P(),
    )
    return jax.shard_map(local, mesh=mesh, in_specs=in_specs, out_specs=out_specs, check_vma=False)
```

```python
import functools

import jax
import jax.numpy as jnp
from jax import lax
from jax.experimental import pallas as pl
from jax.experimental.pallas import tpu as pltpu
from jax.sharding import PartitionSpec as P

BLOCK = 128
MESH = pl.DeviceIdType.MESH


step_size = 0.5
epsilon = 1e-08


def adagrad(table_rows, accum_rows, gradient):
    accum_next = accum_rows + gradient * gradient
    return (table_rows - step_size * gradient / (jnp.sqrt(accum_next) + epsilon), accum_next)


def bit_of(index, weight):
    return lax.rem(lax.div(index, weight), 2)


def flipped(index, weight):
    return index + weight * (1 - 2 * bit_of(index, weight))


def greet(devices):
    barrier = pltpu.get_barrier_semaphore()
    for device in devices:
        pl.semaphore_signal(barrier, inc=1, device_id=device, device_id_type=MESH)
    pl.semaphore_wait(barrier, len(devices))


def chosen(offsets, rows):
    shape = (rows, offsets.shape[1])
    asks = lax.broadcasted_iota(jnp.int32, shape, 0) == jnp.broadcast_to(offsets, shape)
    return jnp.where(asks, 1.0, 0.0).astype(jnp.bfloat16)


def fetch_kernel(n, requests, table, asked_out, returned_out, asked, found, returned, sems):
    me, rep = lax.axis_index("dp"), lax.axis_index("rep")
    peers = [lax.rem(me + j, n) for j in range(1, n)]
    sources = [lax.rem(me + n - j, n) for j in range(1, n)]
    greet([(peer, rep) for peer in peers])
    asking = []
    for j, peer in enumerate(peers):
        copy = pltpu.make_async_remote_copy(
            requests.at[peer], asked.at[me], sems.at[0, j], sems.at[1, j], (peer, rep), MESH
        )
        copy.start()
        asking.append(copy)
    rows = table[...].astype(jnp.bfloat16)

    def rows_of(offsets):
        return lax.dot_general(
            chosen(offsets, rows.shape[0]),
            rows,
            (((0,), (0,)), ((), ())),
            preferred_element_type=jnp.float32,
        ).astype(jnp.bfloat16)

    asked[me] = requests[me]
    returned[me] = rows_of(requests[me])
    answers = []
    for j, source in enumerate(sources):
        asking[j].wait_recv()
        found[j] = rows_of(asked[source])
        copy = pltpu.make_async_remote_copy(
            found.at[j], returned.at[me], sems.at[2, j], sems.at[3, j], (source, rep), MESH
        )
        copy.start()
        answers.append(copy)
    asked_out[...] = asked[...]
    for j in range(n - 1):
        asking[j].wait_send()
        answers[j].wait()
    returned_out[...] = returned[...]


def fetch(requests, table):
    n, cap = requests.shape
    width = table.shape[1]
    vmem = pl.BlockSpec(memory_space=pltpu.VMEM)
    asked, returned = pl.pallas_call(
        functools.partial(fetch_kernel, n),
        out_shape=(
            jax.ShapeDtypeStruct((n, 1, cap), jnp.int32),
            jax.ShapeDtypeStruct((n, cap, width), jnp.bfloat16),
        ),
        in_specs=[vmem] * 2,
        out_specs=(vmem, vmem),
        scratch_shapes=[
            pltpu.VMEM((n, 1, cap), jnp.int32),
            pltpu.VMEM((n - 1, cap, width), jnp.bfloat16),
            pltpu.VMEM((n, cap, width), jnp.bfloat16),
            pltpu.SemaphoreType.DMA((4, n - 1)),
        ],
        compiler_params=pltpu.CompilerParams(collective_id=0, has_side_effects=True),
    )(requests.reshape(n, 1, cap), table)
    return asked, returned


def combine_kernel(
    n, links, top, hot, outgoing, asked, table, accum,
    top_out, hot_out, table_out, accum_out,
    incoming, cold, cold_half, cold_got, cold_last, table_all, accum_all,
    top_got, a_parts, a_gots, b_parts, b_gots, h_parts, h_gots, h_news, sends, recvs,
):
    me, rep = lax.axis_index("dp"), lax.axis_index("rep")
    core, side = bit_of(rep, 1), bit_of(rep, 2)
    over_core, over_side = (me, flipped(rep, 1)), (me, flipped(rep, 2))
    weights = [1 << k for k in range(links)]
    dp_bits = [bit_of(me, weight) for weight in weights]
    over_dp = [(flipped(me, weight), rep) for weight in weights]
    peers = [lax.rem(me + j, n) for j in range(1, n)]
    sources = [lax.rem(me + n - j, n) for j in range(1, n)]
    greet([(peer, rep) for peer in peers] + [over_core, over_side])
    count = [0]

    def send(src, dst, device):
        k = count[0]
        count[0] += 1
        copy = pltpu.make_async_remote_copy(src, dst, sends.at[k], recvs.at[k], device, MESH)
        copy.start()
        return copy

    hot_copy = send(hot.at[:, 1 - core], h_gots[0], over_core)
    top_copy = send(top.at[:, 1 - core], top_got, over_core)
    cold_copies = [
        send(outgoing.at[peer], incoming.at[me], (peer, rep)) for peer in peers
    ]

    a_route = [(side, over_side)] + list(zip(dp_bits, over_dp))
    b_route = [(dp_bits[0], over_dp[0]), (side, over_side)] + list(zip(dp_bits, over_dp))[1:]
    h_route = [(core, over_core)] + a_route

    def step_on(parts, gots, route, k, copy):
        bit = route[k][0]
        copy.wait()
        kept = parts[k][:, bit] + gots[k][...]
        if k + 1 == len(route):
            return kept
        parts[k + 1][...] = kept.reshape(parts[k + 1].shape)
        next_bit, device = route[k + 1]
        return send(parts[k + 1].at[:, 1 - next_bit], gots[k + 1], device)

    all_h = [hot] + list(h_parts)
    hot_state = [0, hot_copy]

    def spread(i):
        bit, device = h_route[len(h_route) - 1 - i]
        cur, new = h_news[2 * i], h_news[2 * i + 1]
        hot_state[1] = send(cur, new.at[:, bit], device)
        new[:, bit] = cur[...]

    def advance_hot():
        k, copy = hot_state
        i = k - len(h_route)
        hot_state[0] = k + 1
        if i >= 0:
            copy.wait()
            if i + 1 < len(h_route):
                cur = h_news[2 * i + 2]
                cur[...] = h_news[2 * i + 1][...].reshape(cur.shape)
                spread(i + 1)
        else:
            result = step_on(all_h, h_gots, h_route, k, copy)
            if i == -1:
                h_news[0][...] = result
                spread(0)
            else:
                hot_state[1] = result

    advance_hot()
    top_copy.wait()
    half = top.shape[3] // 2
    a_parts[0][...] = (top[:, core, :, :half] + top_got[:, :, :half]).reshape(a_parts[0].shape)
    a_copy = send(a_parts[0].at[:, 1 - side], a_gots[0], over_side)
    b_parts[0][...] = (top[:, core, :, half:] + top_got[:, :, half:]).reshape(b_parts[0].shape)
    b_copy = send(b_parts[0].at[:, 1 - dp_bits[0]], b_gots[0], over_dp[0])
    advance_hot()

    own_rows = table.shape[0] * table.shape[1]
    total = jnp.dot(
        chosen(asked[me], own_rows), outgoing[me], preferred_element_type=jnp.float32
    )
    for j, source in enumerate(sources):
        cold_copies[j].wait_recv()
        total += jnp.dot(
            chosen(asked[source], own_rows), incoming[source], preferred_element_type=jnp.float32
        )
    cold[...] = total.reshape(cold.shape)
    cold_copy = send(cold.at[:, 1 - core], cold_got, over_core)
    advance_hot()
    cold_copy.wait()
    cold_half[...] = cold[:, core] + cold_got[...]
    cold_copy = send(cold_half.at[1 - side], cold_last, over_side)
    advance_hot()
    a_copy = step_on(a_parts, a_gots, a_route, 0, a_copy)
    b_copy = step_on(b_parts, b_gots, b_route, 0, b_copy)
    advance_hot()
    cold_copy.wait()
    table_next, accum_next = adagrad(table[rep], accum[rep], cold_half[side] + cold_last[...])
    table_all[side, core] = table_next
    accum_all[side, core] = accum_next
    pair = [send(ref.at[side, core], ref.at[side, core], over_side) for ref in (table_all, accum_all)]
    advance_hot()
    last = len(a_route)
    for k in range(1, last):
        a_copy = step_on(a_parts, a_gots, a_route, k, a_copy)
        b_copy = step_on(b_parts, b_gots, b_route, k, b_copy)
        if k == 1:
            for copy in pair:
                copy.wait()
            pair = [send(ref.at[:, core], ref.at[:, core], over_core) for ref in (table_all, accum_all)]
        if hot_state[0] < 2 * len(h_route):
            advance_hot()
    top_out[:, :half] = a_copy.reshape(top_out.shape[0], half)
    top_out[:, half:] = b_copy.reshape(top_out.shape[0], half)
    for copy in pair:
        copy.wait()
    table_out[...] = table_all[...]
    accum_out[...] = accum_all[...]
    while hot_state[0] < 2 * len(h_route):
        advance_hot()
    hot_out[...] = h_news[-1][...]
    for copy in cold_copies:
        copy.wait_send()


def combine(top, hot, outgoing, asked, table, accum):
    n, cap, width = outgoing.shape
    devices = 4 * n
    links = n.bit_length() - 1
    rows, columns = top.shape[0] // devices, top.shape[1]
    hot_rows = hot.shape[0] // devices
    quarter = table.shape[0] // 4
    half = columns // 2
    f32 = lambda *shape: pltpu.VMEM(shape, jnp.float32)
    steps = [2**k for k in range(links, -1, -1)]
    a_parts = [f32(m, 2, rows, half) for m in steps]
    a_gots = [f32(m, rows, half) for m in steps]
    b_parts = [f32(n // 2, 2, 2, rows, half), f32(n // 2, 2, rows, half)] + a_parts[2:]
    b_gots = [f32(n // 2, 2, rows, half), f32(n // 2, rows, half)] + a_gots[2:]
    h_parts = [f32(m, 2, hot_rows, width) for m in steps]
    h_gots = [f32(m, hot_rows, width) for m in [2 * n] + steps]
    h_news = []
    for m in steps[::-1] + [2 * n]:
        h_news += [f32(m, hot_rows, width), f32(m, 2, hot_rows, width)]
    copies = 1 + (n - 1) + 2 * (links + 1) + 2 * (links + 2) + 2 + 4
    vmem = pl.BlockSpec(memory_space=pltpu.VMEM)
    out = lambda *shape: jax.ShapeDtypeStruct(shape, jnp.float32)
    square = (2, 2, quarter, width)
    return pl.pallas_call(
        functools.partial(combine_kernel, n, links),
        out_shape=(
            out(rows, columns), out(2 * n, 2, hot_rows, width), out(*square), out(*square)
        ),
        in_specs=[vmem] * 6,
        out_specs=(vmem,) * 4,
        scratch_shapes=[
            pltpu.VMEM((n, cap, width), jnp.bfloat16),
            f32(*square),
            f32(2, quarter, width),
            f32(2, quarter, width),
            f32(quarter, width),
            f32(*square),
            f32(*square),
            f32(2 * n, rows, columns),
            a_parts, a_gots, b_parts, b_gots, h_parts, h_gots, h_news,
            pltpu.SemaphoreType.DMA((copies,)),
            pltpu.SemaphoreType.DMA((copies,)),
        ],
        compiler_params=pltpu.CompilerParams(collective_id=1, has_side_effects=True),
    )(
        top.reshape(2 * n, 2, rows, columns),
        hot.reshape(2 * n, 2, hot_rows, width),
        outgoing, asked,
        table.reshape(4, quarter, width),
        accum.reshape(4, quarter, width),
    )


def suits(n, rep_n, top_rows):
    return rep_n == 4 and n >= 2 and n & (n - 1) == 0 and top_rows % (8 * n * rep_n) == 0


def local(
    hot_ids,
    cold_owner,
    cold_offset,
    labels,
    top_weight,
    out_weight,
    cold_table,
    cold_accum,
    hot_cache,
    hot_accum,
    pending,
    refresh_blocks,
    block_clock,
):
    width = hot_cache.shape[1]
    samples = hot_ids.shape[0]
    hot_feats = hot_ids.shape[1]
    lookups = cold_offset.shape[0]
    cold_feats = lookups // samples
    owners_count = lax.axis_size("dp")
    capacity = max(2, 2 * lookups // owners_count)
    owners = cold_owner[:, 0]
    matches = (owners[:, None] == jnp.arange(owners_count, dtype=jnp.int32)[None, :]).astype(
        jnp.int32
    )
    before = jnp.arange(lookups)[:, None] > jnp.arange(lookups)[None, :]
    earlier = jnp.dot(
        before.astype(jnp.bfloat16),
        matches.astype(jnp.bfloat16),
        preferred_element_type=jnp.float32,
    ).astype(jnp.int32)
    positions = jnp.sum(earlier * matches, axis=1)
    targets = owners * capacity + positions
    places = jnp.arange(owners_count * capacity, dtype=jnp.int32)
    placed = targets[:, None] == places[None, :]
    requests = jnp.sum(jnp.where(placed, cold_offset[:, None], 0), axis=0)
    placed = placed.astype(jnp.bfloat16)
    requests = requests.reshape(owners_count, capacity)
    direct = suits(owners_count, lax.axis_size("rep"), top_weight.shape[0])
    if direct:
        asked, returned = fetch(requests, cold_table)
    else:
        asked = lax.all_to_all(requests, "dp", split_axis=0, concat_axis=0, tiled=True)
        found = cold_table[asked].astype(jnp.bfloat16)
        returned = lax.all_to_all(found, "dp", split_axis=0, concat_axis=0, tiled=True)
    cold_rows = jnp.dot(
        placed,
        returned.reshape(owners_count * capacity, width),
        preferred_element_type=jnp.float32,
    ).astype(jnp.bfloat16)
    cold_rows = cold_rows.reshape(samples, cold_feats, width)
    hot_rows = hot_cache[hot_ids].astype(jnp.bfloat16)
    inputs = jnp.concatenate([hot_rows, cold_rows], axis=1).reshape(
        samples, (hot_feats + cold_feats) * width
    )
    preact = jnp.dot(inputs, top_weight, preferred_element_type=jnp.float32)
    hidden = jax.nn.silu(preact).astype(jnp.bfloat16)
    hidden_wide = hidden.astype(jnp.float32)
    logits = jnp.dot(hidden_wide, out_weight, precision=lax.Precision.HIGHEST)
    errors = jax.nn.sigmoid(logits) - labels.astype(jnp.float32)
    gates = jax.nn.sigmoid(preact)
    slope = gates * (1.0 + preact * (1.0 - gates))
    dhidden = (errors[:, None] * out_weight[None, :] * slope).astype(jnp.bfloat16)
    head_term = jnp.dot(errors, hidden_wide, precision=lax.Precision.HIGHEST)
    top_part = lax.dot_general(
        inputs, dhidden, (((0,), (0,)), ((), ())), preferred_element_type=jnp.float32
    )
    dinputs = lax.dot_general(
        dhidden, top_weight, (((1,), (1,)), ((), ())), preferred_element_type=jnp.float32
    ).astype(jnp.bfloat16)
    dinputs = dinputs.reshape(samples, hot_feats + cold_feats, width)
    cold_dx = dinputs[:, hot_feats:].reshape(lookups, width)
    outgoing = lax.dot_general(
        placed, cold_dx, (((0,), (0,)), ((), ())), preferred_element_type=jnp.float32
    ).astype(jnp.bfloat16)
    outgoing = outgoing.reshape(owners_count, capacity, width)
    own_rows = cold_table.shape[0]
    quarter = own_rows // lax.axis_size("rep")
    hot_count = hot_cache.shape[0]
    blocks_count = hot_count // BLOCK
    hot_dx = dinputs[:, :hot_feats].reshape(samples * hot_feats, width)
    hot_named = (
        jnp.arange(hot_count, dtype=jnp.int32)[:, None] == hot_ids.reshape(-1)[None, :]
    ).astype(jnp.bfloat16)
    hot_grad = jnp.dot(hot_named, hot_dx, preferred_element_type=jnp.float32)
    carried = (pending + hot_grad).reshape(blocks_count, BLOCK, width)
    picked = carried[refresh_blocks]
    divisors = 1.0 + block_clock.astype(jnp.float32)
    named = refresh_blocks[:, None] == jnp.arange(blocks_count, dtype=jnp.int32)[None, :]
    refreshed = jnp.any(named, axis=0)[:, None, None]
    cache_blocks = hot_cache.reshape(blocks_count, BLOCK, width)
    accum_blocks = hot_accum.reshape(blocks_count, BLOCK, width)
    if direct:
        picked_rows = refresh_blocks.shape[0] * BLOCK
        head_rows = head_term.shape[0] // width
        even = 8 * owners_count * lax.axis_size("rep")
        spare = -(picked_rows + head_rows) % even
        summands = jnp.concatenate(
            [
                picked.reshape(picked_rows, width),
                head_term.reshape(head_rows, width),
                jnp.zeros((spare, width), jnp.float32),
            ]
        )
        top_grad, sums, cold_table_new, cold_accum_new = combine(
            top_part, summands, outgoing, asked, cold_table, cold_accum
        )
        cold_table_new = cold_table_new.reshape(own_rows, width)
        cold_accum_new = cold_accum_new.reshape(own_rows, width)
        sums = sums.reshape(-1, width)
        picked_sum = sums[:picked_rows].reshape(picked.shape)
        out_grad = sums[picked_rows : picked_rows + head_rows].reshape(-1)
    else:
        incoming = lax.all_to_all(outgoing, "dp", split_axis=0, concat_axis=0, tiled=True)
        cold_grad = (
            jnp.zeros((own_rows, width), jnp.float32)
            .at[asked.reshape(-1)]
            .add(incoming.reshape(-1, width).astype(jnp.float32))
        )
        cold_share = lax.psum_scatter(cold_grad, "rep", scatter_dimension=0, tiled=True)
        offset_rows = lax.axis_index("rep") * quarter
        table_share = lax.dynamic_slice_in_dim(cold_table, offset_rows, quarter, 0)
        accum_share = lax.dynamic_slice_in_dim(cold_accum, offset_rows, quarter, 0)
        table_updated, accum_updated = adagrad(table_share, accum_share, cold_share)
        cold_table_new, cold_accum_new = (
            lax.all_gather(table_updated, "rep", axis=0, tiled=True),
            lax.all_gather(accum_updated, "rep", axis=0, tiled=True),
        )
        top_grad = lax.psum_scatter(top_part, ("dp", "rep"), scatter_dimension=0, tiled=True)
        picked_sum, out_grad = lax.psum((picked, head_term), ("dp", "rep"))
    block_sums = jnp.zeros((), jnp.float32)
    for k in range(refresh_blocks.shape[0]):
        block_sums = jnp.where(named[k][:, None, None], picked_sum[k][None], block_sums)
    flush = block_sums / divisors[:, None, None]
    cache_next, accum_next = adagrad(cache_blocks, accum_blocks, flush)
    hot_cache_new = jnp.where(refreshed, cache_next, cache_blocks).reshape(hot_count, width)
    hot_accum_new = jnp.where(refreshed, accum_next, accum_blocks).reshape(hot_count, width)
    pending_new = jnp.where(refreshed, 0.0, carried).reshape(hot_count, width)
    return (
        cold_table_new,
        cold_accum_new,
        hot_cache_new,
        hot_accum_new,
        pending_new,
        top_grad,
        out_grad,
    )


def solution(mesh):
    in_specs = (
        P(("dp", "rep"), None),
        P(("dp", "rep"), None),
        P(("dp", "rep")),
        P(("dp", "rep")),
        P(),
        P(),
        P("dp", None),
        P("dp", None),
        P(),
        P(),
        P(("dp", "rep"), None),
        P(),
        P(),
    )
    out_specs = (
        P("dp", None),
        P("dp", None),
        P(),
        P(),
        P(("dp", "rep"), None),
        P(("dp", "rep"), None),
        P(),
    )
    return jax.shard_map(local, mesh=mesh, in_specs=in_specs, out_specs=out_specs, check_vma=False)
```
